128 devices in a mesh: energy: 64 (over x, z_lo, y, core), slab: 2 (over z_hi).
Axes of the slice: x: 4, y: 4, z: 4 (z_hi: 2, z_lo: 2; z = z_hi * 2 + z_lo), core: 2. Of those that a mesh axis runs over, the one named last changes fastest.
Arguments:
- retarded: bfloat16 [64, 4, 5, 2, 384, 384], P('energy', 'slab'), may hold values from -0.09375 to 0.09375
- ballistic: float32 [64, 4, 2, 384, 384], P('energy', 'slab'), may hold values from -6 to 6
- coupling: bfloat16 [2, 384, 384], replicated, may hold values from -0.3125 to 0.3125
- occupation: float32 [2], replicated, may hold values from 0.2 to 2
- shifts: int32 [2], replicated, may hold values from 1 to 2, as said below
Outputs:
- lesser: float32 [64, 4, 2, 384, 384], P('energy', 'slab')
The draws below stay inside these ranges and needn't reach their ends.
Inputs may be any that keep to these rules, and one draw needn't show every extreme that they name: The modes' shifts are the numbers 1 to 2 in some order.
All inputs are finite; a program needn't handle non-finite values.
Results may differ from the reference program's by a relative error of at most 0.012.
Values may be sent and summed in bfloat16 or wider, within the bound.
No kernel may reach another device: no remote copies, remote signals or barrier semaphores. Data moves between devices by JAX's collectives and lax.ppermute only.
A program may use at most 128 MiB of HBM per device.

```python
import math
import jax
import jax.numpy as jnp
from jax import lax

B = 384
MODES = 2
ITERS = 2
NE = 64
NBLK = 4


def draw_shifts(key, part):
    return jax.random.permutation(jax.random.fold_in(key, 17), jnp.arange(1, MODES + 1, dtype=jnp.int32)).astype(jnp.int32)


def level_of(own_key, shape, cuts, smallest, top_value):
    def one(axis_at, shards_of):
        steps = jax.random.uniform(jax.random.fold_in(jax.random.fold_in(own_key, 6), axis_at), (shards_of,), jnp.float32, smallest / len(cuts), top_value / len(cuts))
        return jnp.repeat(jnp.exp(steps), shape[axis_at] // shards_of).reshape((-1,) + (1,) * (len(shape) - axis_at - 1))

    loudness = one(*cuts[0])
    for cut in cuts[1:]:
        loudness = loudness * one(*cut)
    return loudness


def noise(own_key, shape, deviation, limit, cuts=(), kind=jnp.bfloat16):
    loudness = level_of(own_key, shape, cuts, -0.22, 0.18) if cuts else 1.0
    values = jax.random.normal(own_key, shape, jnp.float32) * deviation * loudness
    return jnp.minimum(jnp.maximum(values, -limit), limit).astype(kind)


def setup_inputs(seed: int = 0) -> dict:
    splits = jax.random.split(jax.random.key(seed), 6)
    return {
        "retarded": noise(splits[0], (NE, NBLK, 5, 2, B, B), (10 * B) ** -0.5, 0.09375, ((0, 64), (1, 2))),
        "ballistic": noise(splits[1], (NE, NBLK, 2, B, B), 1.0, 6.0, ((0, 64), (1, 2)), jnp.float32),
        "coupling": noise(splits[2], (MODES, B, B), B ** -0.5, 0.3125),
        "occupation": jnp.clip(jnp.exp(jax.random.uniform(splits[3], (MODES,), jnp.float32, math.log(0.2), math.log(2.0))), 0.2, 2.0),
        "shifts": draw_shifts(jax.random.fold_in(splits[5], 71), 0),
    }


def reference(retarded, ballistic, coupling, occupation, shifts):
    energies = ballistic.shape[0]
    blocks = ballistic.shape[1]
    highest = lax.Precision.HIGHEST
    weights = coupling.astype(jnp.float32)
    current = ballistic
    for iteration in range(ITERS):
        rounded = lax.optimization_barrier(current.astype(jnp.bfloat16)).astype(jnp.float32)
        padded = jnp.pad(rounded, ((MODES, MODES), (0, 0), (0, 0), (0, 0), (0, 0)))
        scatter_total = jnp.zeros_like(current)
        for mode in range(MODES):
            rising = lax.dynamic_slice_in_dim(padded, (MODES + shifts[mode]).astype(jnp.int32), energies, 0)
            falling = lax.dynamic_slice_in_dim(padded, (MODES - shifts[mode]).astype(jnp.int32), energies, 0)
            mixture = (1.0 + occupation[mode]) * rising + occupation[mode] * falling
            mixture = lax.optimization_barrier(mixture.astype(jnp.bfloat16)).astype(jnp.float32)
            inner = jnp.einsum('ab,enrbc->enrac', weights[mode], mixture, precision=highest)
            inner = lax.optimization_barrier(inner.astype(jnp.bfloat16)).astype(jnp.float32)
            scatter_total = scatter_total + jnp.einsum('enrab,cb->enrac', inner, weights[mode], precision=highest)
        scatter_round = lax.optimization_barrier(scatter_total.astype(jnp.bfloat16)).astype(jnp.float32)
        scatter_pad = jnp.pad(scatter_round, ((0, 0), (2, 2), (0, 0), (0, 0), (0, 0)))

        def one_energy(items):
            band, around, source = items
            band = band.astype(jnp.float32)
            nearby = jnp.stack([around[offset:offset + blocks] for offset in range(5)], axis=1)
            ret_real = band[:, :, 0]
            ret_imag = band[:, :, 1]
            near_real = nearby[:, :, 0]
            near_imag = nearby[:, :, 1]
            pattern = 'njab,njbc->njac'
            left_real = jnp.einsum(pattern, ret_real, near_real, precision=highest) - jnp.einsum(pattern, ret_imag, near_imag, precision=highest)
            left_imag = jnp.einsum(pattern, ret_real, near_imag, precision=highest) + jnp.einsum(pattern, ret_imag, near_real, precision=highest)
            left_real = lax.optimization_barrier(left_real.astype(jnp.bfloat16)).astype(jnp.float32)
            left_imag = lax.optimization_barrier(left_imag.astype(jnp.bfloat16)).astype(jnp.float32)
            closing = 'njab,njcb->nac'
            out_real = jnp.einsum(closing, left_real, ret_real, precision=highest) + jnp.einsum(closing, left_imag, ret_imag, precision=highest)
            out_imag = jnp.einsum(closing, left_imag, ret_real, precision=highest) - jnp.einsum(closing, left_real, ret_imag, precision=highest)
            return source + jnp.stack([out_real, out_imag], axis=1)

        current = lax.map(one_energy, (retarded, scatter_pad, ballistic))
    return current
```

```python
import jax
import jax.numpy as jnp
from jax import lax
from jax.experimental import pallas as pl
from jax.experimental.pallas import tpu as pltpu
from jax.sharding import PartitionSpec as P

ITERS = 2
B = 384
PAIRS = 7
F32 = jnp.float32
BF16 = jnp.bfloat16

VMEM = pl.BlockSpec(memory_space=pltpu.VMEM)
SMEM = pl.BlockSpec(memory_space=pltpu.SMEM)
ANY = pl.BlockSpec(memory_space=pl.ANY)
PLANE = (B, 2 * B)
SQUARE = (2 * B, 2 * B)


def dot(a, b):
    return jnp.dot(a, b, preferred_element_type=F32)


def call(body, outs, operands, specs, flops, moved, limit, scratch=()):
    return pl.pallas_call(
        body,
        out_shape=outs,
        in_specs=specs,
        out_specs=jax.tree.map(lambda _: VMEM, outs),
        scratch_shapes=scratch,
        compiler_params=pltpu.CompilerParams(vmem_limit_bytes=limit << 20),
        cost_estimate=pl.CostEstimate(flops=flops, bytes_accessed=moved, transcendentals=0),
    )(*operands)


def plane(dtype):
    return jax.ShapeDtypeStruct(PLANE, dtype)


def round_body(ballistic, near, far):
    slab = lax.axis_index("slab")
    for part in range(2):
        columns = slice(part * B, part * B + B)
        near[:, columns] = ballistic[0, 1 - slab, part].astype(BF16)
        far[:, columns] = ballistic[0, slab, part].astype(BF16)


def prepare_body(retarded, coupling, shifts, rows, turned, weights, weights_turned, buffer, sems):
    slab = lax.axis_index("slab")
    away = 1 - 2 * slab
    places = (
        (slab, 2),
        (slab, 2 + away),
        (1 - slab, 2 - away),
        (1 - slab, 2),
        (slab, 2 + 2 * away),
        (1 - slab, 2 + away),
        (1 - slab, 2 + 2 * away),
    )
    copies = [
        pltpu.make_async_copy(retarded.at[0, i, j], buffer.at[t], sems.at[t])
        for t, (i, j) in enumerate(places)
    ]
    for copy in copies:
        copy.start()
    first = jnp.where(shifts[0] == 1, 0, 1)
    for at, mode in enumerate((first, 1 - first)):
        matrix = coupling[mode]
        weights[at] = matrix
        weights_turned[at * B : at * B + B, :] = matrix.T
    for t, copy in enumerate(copies):
        copy.wait()
        real = buffer[t, 0]
        imag = buffer[t, 1]
        rows[t, :, :B] = real
        rows[t, :, B:] = imag
        real = real.T
        imag = imag.T
        turned[t, :B, :B] = real
        turned[t, B:, :B] = imag
        turned[t, :B, B:] = -imag
        turned[t, B:, B:] = real


def scatter_body(own, relayed, early, late, weights, weights_turned, occupation, shifts, out):
    core = lax.rem(lax.axis_index("energy"), 2)
    first = jnp.where(shifts[0] == 1, 0, 1)
    one = occupation[first]
    two = occupation[1 - first]
    up = jnp.where(core == 0, 1.0, 0.0)
    down = 1.0 - up
    mixed = (own[...].astype(F32) * (one + up) + relayed[...].astype(F32) * (one + down)).astype(BF16)
    inner_one = dot(weights[0], mixed).astype(BF16)
    mixed = (early[...].astype(F32) * (two + up) + late[...].astype(F32) * (two + down)).astype(BF16)
    inner_two = dot(weights[1], mixed).astype(BF16)
    for part in range(2):
        columns = slice(part * B, part * B + B)
        inner = jnp.concatenate([inner_one[:, columns], inner_two[:, columns]], axis=1)
        out[:, columns] = dot(inner, weights_turned[...]).astype(BF16)


def spread(scattering, full):
    real = scattering[:, :B]
    imag = scattering[:, B:]
    full[:B, :B] = real
    full[:B, B:] = imag
    full[B:, :B] = -imag
    full[B:, B:] = real


def term(rows, full, turned):
    return dot(dot(rows, full[...]).astype(BF16), turned)


def local_body(ballistic, near, far, rows, turned, out_near, out_far, full):
    slab = lax.axis_index("slab")
    for part in range(2):
        columns = slice(part * B, part * B + B)
        out_near[:, columns] = ballistic[0, 1 - slab, part]
        out_far[:, columns] = ballistic[0, slab, part]
    spread(near, full)
    out_near[...] += term(rows[3], full, turned[3])
    out_far[...] += term(rows[1], full, turned[1])
    spread(far, full)
    out_near[...] += term(rows[2], full, turned[2])
    out_far[...] += term(rows[0], full, turned[0])


def pair_body(t, total, scattering, rows, turned, out, full):
    spread(scattering, full)
    out[...] = (total[...] + term(rows[t], full, turned[t])).astype(out.dtype)


def last_body(near, far, scattering, rows, turned, out, full):
    slab = lax.axis_index("slab")
    spread(scattering, full)
    for t, total, place in ((4, far, slab), (5, near, 1 - slab)):
        result = total[...] + term(rows[t], full, turned[t])
        out[0, place, 0] = result[:, :B]
        out[0, place, 1] = result[:, B:]


def shards(retarded, ballistic, coupling, occupation, shifts):
    energies = lax.axis_size("energy")
    flops = 2 * B * 4 * B * B

    def moves(even, odd):
        steps = [(e, e + (odd if e % 2 else even)) for e in range(energies)]
        return [(a, b) for a, b in steps if 0 <= b < energies]

    early_moves = moves(-2, 2)
    late_moves = moves(2, -2)
    swap_moves = moves(1, -1)

    def exchange(block):
        early = lax.ppermute(block, "energy", early_moves)
        late = lax.ppermute(block, "energy", late_moves)
        own = lax.ppermute(block, "energy", swap_moves)
        relayed = lax.ppermute(early, "energy", swap_moves)
        return own, relayed, early, late

    def scatter(parts):
        return call(
            scatter_body,
            plane(BF16),
            (*parts, weights, weights_turned, occupation, shifts),
            [VMEM] * 6 + [SMEM] * 2,
            2 * flops,
            6 << 20,
            16,
        )

    def across(block):
        return lax.ppermute(block, "slab", [(0, 1), (1, 0)])

    def pair(t, total, scattering, dtype):
        return call(
            lambda *refs: pair_body(t, *refs),
            plane(dtype),
            (total, scattering, rows, turned),
            [VMEM] * 4,
            2 * flops,
            4 << 20,
            40,
            [pltpu.VMEM(SQUARE, BF16)],
        )

    near, far = call(
        round_body, [plane(BF16), plane(BF16)], (ballistic,), [VMEM], 0, 4 << 20, 16
    )
    rows, turned, weights, weights_turned = call(
        prepare_body,
        [
            jax.ShapeDtypeStruct((PAIRS, *PLANE), BF16),
            jax.ShapeDtypeStruct((PAIRS, *SQUARE), BF16),
            jax.ShapeDtypeStruct((2, B, B), BF16),
            jax.ShapeDtypeStruct((2 * B, B), BF16),
        ],
        (retarded, coupling, shifts),
        [ANY, VMEM, SMEM],
        0,
        20 << 20,
        40,
        [pltpu.VMEM((PAIRS, 2, B, B), BF16), pltpu.SemaphoreType.DMA((PAIRS,))],
    )
    for iteration in range(ITERS):
        if iteration == 0:
            parts_near = exchange(near)
            parts_far = exchange(far)
        else:
            parts_far = exchange(far)
            parts_near = exchange(near)
        scatter_near = scatter(parts_near)
        scatter_far = scatter(parts_far)
        other_near = across(scatter_near)
        other_far = across(scatter_far)
        total_near, total_far = call(
            local_body,
            [plane(F32), plane(F32)],
            (ballistic, scatter_near, scatter_far, rows, turned),
            [VMEM] * 5,
            8 * flops,
            14 << 20,
            40,
            [pltpu.VMEM(SQUARE, BF16)],
        )
        if iteration == 0:
            far = pair(4, total_far, other_near, BF16)
            total_near = pair(5, total_near, other_near, F32)
            near = pair(6, total_near, other_far, BF16)
        else:
            total_near = pair(6, total_near, other_far, F32)
            return call(
                last_body,
                jax.ShapeDtypeStruct(ballistic.shape, F32),
                (total_near, total_far, other_near, rows, turned),
                [VMEM] * 5,
                4 * flops,
                8 << 20,
                40,
                [pltpu.VMEM(SQUARE, BF16)],
            )


def solution(mesh):
    return jax.shard_map(
        shards,
        mesh=mesh,
        in_specs=(
            P("energy", "slab", None, None, None, None),
            P("energy", "slab", None, None, None),
            P(),
            P(),
            P(),
        ),
        out_specs=P("energy", "slab", None, None, None),
        check_vma=False,
    )
```

```python
import jax
import jax.numpy as jnp
from jax import lax
from jax.experimental import pallas as pl
from jax.experimental.pallas import tpu as pltpu
from jax.sharding import PartitionSpec as P


B = 384
F32 = jnp.float32
BF16 = jnp.bfloat16


VMEM = pl.BlockSpec(memory_space=pltpu.VMEM)
SMEM = pl.BlockSpec(memory_space=pltpu.SMEM)
HBM = pl.BlockSpec(memory_space=pltpu.HBM)
PLANE = (B, 2 * B)
SQUARE = (2 * B, 2 * B)


def dot(a, b):
    return jnp.dot(a, b, preferred_element_type=F32)


def call(body, outs, operands, specs, flops, moved, limit, scratch=(), out_spec=VMEM):
    return pl.pallas_call(
        body,
        out_shape=outs,
        in_specs=specs,
        out_specs=jax.tree.map(lambda _: out_spec, outs),
        scratch_shapes=scratch,
        compiler_params=pltpu.CompilerParams(vmem_limit_bytes=limit << 20),
        cost_estimate=pl.CostEstimate(flops=flops, bytes_accessed=moved, transcendentals=0),
    )(*operands)


def plane(dtype):
    return jax.ShapeDtypeStruct(PLANE, dtype)


def round_body(is_near, ballistic, out, buffer, sems):
    slab = lax.axis_index("slab")
    block = 1 - slab if is_near else slab
    copies = [
        pltpu.make_async_copy(ballistic.at[0, block, part], buffer.at[part], sems.at[part])
        for part in range(2)
    ]
    for copy in copies:
        copy.start()
    for part, copy in enumerate(copies):
        copy.wait()
        out[:, part * B : part * B + B] = buffer[part].astype(BF16)


def weights_body(coupling, occupation, shifts, weights, weights_turned, factors):
    energy = lax.axis_index("energy")
    last_energy = lax.axis_size("energy") - 1
    toward = 1 - 2 * lax.rem(energy, 2)
    first = jnp.where(shifts[0] == 1, 0, 1)
    for at, mode in enumerate((first, 1 - first)):
        matrix = coupling[mode]
        weights[at] = matrix
        weights_turned[at * B : at * B + B, :] = matrix.T
        for side in range(2):
            offset = (1 - 2 * side) * (at + 1) * toward
            factor = occupation[mode] + jnp.where(offset > 0, 1.0, 0.0)
            inside = (energy + offset >= 0) & (energy + offset <= last_energy)
            factor = jnp.where(inside, factor, 0.0)
            factors[2 * at + side : 2 * at + side + 1, :] = jnp.full((1, 2 * B), factor, F32)


def prepare_body(pairs, retarded, *refs):
    count = len(pairs)
    rows, turned, buffer, sems = refs[:count], refs[count : 2 * count], refs[-2], refs[-1]
    slab = lax.axis_index("slab")
    away = 1 - 2 * slab
    places = (
        (slab, 2),
        (slab, 2 + away),
        (1 - slab, 2 - away),
        (1 - slab, 2),
        (slab, 2 + 2 * away),
        (1 - slab, 2 + away),
        (1 - slab, 2 + 2 * away),
    )
    copies = []
    for at, t in enumerate(pairs):
        i, j = places[t]
        copies.append(pltpu.make_async_copy(retarded.at[0, i, j], buffer.at[at], sems.at[at]))
        copies[-1].start()
    for at, copy in enumerate(copies):
        copy.wait()
        real = buffer[at, 0]
        imag = buffer[at, 1]
        rows[at][:, :B] = real
        rows[at][:, B:] = imag
        real = real.T
        imag = imag.T
        turned[at][:B, :B] = real
        turned[at][B:, :B] = imag
        turned[at][:B, B:] = -imag
        turned[at][B:, B:] = real


def scatter_body(own, early, relayed, late, weights, weights_turned, factors, out):
    def mixture(first, second, at):
        one = first[...].astype(F32) * factors[at : at + 1, :]
        return (one + second[...].astype(F32) * factors[at + 1 : at + 2, :]).astype(BF16)

    inner_one = dot(weights[0], mixture(own, early, 0)).astype(BF16)
    inner_two = dot(weights[1], mixture(relayed, late, 2)).astype(BF16)
    for part in range(2):
        columns = slice(part * B, part * B + B)
        inner = jnp.concatenate([inner_one[:, columns], inner_two[:, columns]], axis=1)
        out[:, columns] = dot(inner, weights_turned[...]).astype(BF16)


def spread(scattering, full):
    real = scattering[:, :B]
    imag = scattering[:, B:]
    full[:B, :B] = real
    full[:B, B:] = imag
    full[B:, :B] = -imag
    full[B:, B:] = real


def term(rows, full, turned):
    return dot(dot(rows, full[...]).astype(BF16), turned)


def local_body(ballistic, near, far, *refs):
    rows, turned, (out_near, out_far, full) = refs[:4], refs[4:8], refs[8:]
    slab = lax.axis_index("slab")
    for part in range(2):
        columns = slice(part * B, part * B + B)
        out_near[:, columns] = ballistic[0, 1 - slab, part]
        out_far[:, columns] = ballistic[0, slab, part]
    spread(near, full)
    out_near[...] += term(rows[3][...], full, turned[3][...])
    out_far[...] += term(rows[1][...], full, turned[1][...])
    spread(far, full)
    out_near[...] += term(rows[2][...], full, turned[2][...])
    out_far[...] += term(rows[0][...], full, turned[0][...])


def pair_body(total, scattering, rows, turned, out, full):
    spread(scattering, full)
    out[...] = (total[...] + term(rows[...], full, turned[...])).astype(out.dtype)


def last_body(near, far, scattering, rows_far, turned_far, rows_near, turned_near, out, full, results, sems):
    slab = lax.axis_index("slab")
    spread(scattering, full)
    copies = []
    for at, (total, rows, turned, place) in enumerate(
        ((far, rows_far, turned_far, slab), (near, rows_near, turned_near, 1 - slab))
    ):
        result = total[...] + term(rows[...], full, turned[...])
        for part in range(2):
            results[at, part] = result[:, part * B : part * B + B]
            copies.append(
                pltpu.make_async_copy(
                    results.at[at, part], out.at[0, place, part], sems.at[at, part]
                )
            )
            copies[-1].start()
    for copy in copies:
        copy.wait()


def shards(retarded, ballistic, coupling, occupation, shifts):
    energies = lax.axis_size("energy")
    flops = 2 * B * 4 * B * B

    last_energy = energies - 1
    chip_moves = [(e, e ^ 1) for e in range(energies)]
    link_moves = [(e, (e - 1 ^ 1) + 1) for e in range(1, last_energy)]
    link_moves += [(0, last_energy), (last_energy, 0)]

    def shifted(block, pairs):
        return lax.ppermute(block, "energy", pairs)

    def exchange(block):
        own = shifted(block, chip_moves)
        early = shifted(block, link_moves)
        late = shifted(own, link_moves)
        relayed = shifted(early, chip_moves)
        return own, early, relayed, late

    def scatter(*parts):
        return call(
            scatter_body,
            plane(BF16),
            (*parts, weights, weights_turned, factors),
            [VMEM] * 7,
            2 * flops,
            6 << 20,
            12,
        )

    def across(block):
        return lax.ppermute(block, "slab", [(0, 1), (1, 0)])

    def pair(t, total, scattering, dtype):
        return call(
            pair_body,
            plane(dtype),
            (total, scattering, rows[t], turned[t]),
            [VMEM] * 4,
            2 * flops,
            4 << 20,
            12,
            [pltpu.VMEM(SQUARE, BF16)],
        )

    def prepare(pairs):
        count = len(pairs)
        done = call(
            lambda *refs: prepare_body(pairs, *refs),
            [plane(BF16)] * count + [jax.ShapeDtypeStruct(SQUARE, BF16)] * count,
            (pltpu.with_memory_space_constraint(retarded, pltpu.HBM),),
            [HBM],
            0,
            3 * count << 20,
            16,
            [pltpu.VMEM((count, 2, B, B), BF16), pltpu.SemaphoreType.DMA((count,))],
        )
        return done[:count], done[count:]

    def rounded(is_near):
        return call(
            lambda *refs: round_body(is_near, *refs),
            plane(BF16),
            (pltpu.with_memory_space_constraint(ballistic, pltpu.HBM),),
            [HBM],
            0,
            2 << 20,
            4,
            [pltpu.VMEM((2, B, B), F32), pltpu.SemaphoreType.DMA((2,))],
        )

    def weigh():
        return call(
            weights_body,
            [
                jax.ShapeDtypeStruct((2, B, B), BF16),
                jax.ShapeDtypeStruct((2 * B, B), BF16),
                jax.ShapeDtypeStruct((4, 2 * B), F32),
            ],
            (coupling, occupation, shifts),
            [VMEM, SMEM, SMEM],
            0,
            4 << 20,
            4,
        )

    def local(near, far):
        return call(
            local_body,
            [plane(F32), plane(F32)],
            (ballistic, near, far, *rows[:4], *turned[:4]),
            [VMEM] * 11,
            8 * flops,
            14 << 20,
            20,
            [pltpu.VMEM(SQUARE, BF16)],
        )

    def last(near, far, scattering):
        return call(
            last_body,
            jax.ShapeDtypeStruct(ballistic.shape, F32),
            (near, far, scattering, rows[4], turned[4], rows[5], turned[5]),
            [VMEM] * 7,
            4 * flops,
            8 << 20,
            20,
            [
                pltpu.VMEM(SQUARE, BF16),
                pltpu.VMEM((2, 2, B, B), F32),
                pltpu.SemaphoreType.DMA((2, 2)),
            ],
            HBM,
        )

    near = rounded(True)
    far = rounded(False)
    weights, weights_turned, factors = weigh()
    rows, turned = prepare((0, 1, 2, 3))
    more_rows, more_turned = prepare((4, 5, 6))
    rows, turned = rows + more_rows, turned + more_turned
    for tag in ("0", "1"):
        near_parts = exchange(near)
        far_parts = exchange(far)
        scatter_near = scatter(*near_parts)
        scatter_far = scatter(*far_parts)
        other_near = across(scatter_near)
        other_far = across(scatter_far)
        total_near, total_far = local(scatter_near, scatter_far)
        if tag == "0":
            far = pair(4, total_far, other_near, BF16)
            total_near = pair(5, total_near, other_near, F32)
            near = pair(6, total_near, other_far, BF16)
        else:
            total_near = pair(6, total_near, other_far, F32)
            return last(total_near, total_far, other_near)


def solution(mesh):
    return jax.shard_map(
        shards,
        mesh=mesh,
        in_specs=(
            P("energy", "slab", None, None, None, None),
            P("energy", "slab", None, None, None),
            P(),
            P(),
            P(),
        ),
        out_specs=P("energy", "slab", None, None, None),
        check_vma=False,
    )
```

```python
import jax
import jax.numpy as jnp
from jax import lax
from jax.experimental import pallas as pl
from jax.experimental.pallas import tpu as pltpu
from jax.sharding import PartitionSpec as P


B = 384
F32 = jnp.float32
BF16 = jnp.bfloat16


VMEM = pl.BlockSpec(memory_space=pltpu.VMEM)
SMEM = pl.BlockSpec(memory_space=pltpu.SMEM)
HBM = pl.BlockSpec(memory_space=pltpu.HBM)
PLANE = (B, 2 * B)
SQUARE = (2 * B, 2 * B)


def dot(a, b):
    return jnp.dot(a, b, preferred_element_type=F32)


def call(body, outs, operands, specs, flops, moved, limit, scratch=()):
    return pl.pallas_call(
        body,
        out_shape=outs,
        in_specs=specs,
        out_specs=jax.tree.map(lambda _: VMEM, outs),
        scratch_shapes=scratch,
        compiler_params=pltpu.CompilerParams(vmem_limit_bytes=limit << 20),
        cost_estimate=pl.CostEstimate(flops=flops, bytes_accessed=moved, transcendentals=0),
    )(*operands)


def plane(dtype):
    return jax.ShapeDtypeStruct(PLANE, dtype)


def round_body(is_near, ballistic, out, buffer, sems):
    slab = lax.axis_index("slab")
    block = 1 - slab if is_near else slab
    copies = [
        pltpu.make_async_copy(ballistic.at[0, block, part], buffer.at[part], sems.at[part])
        for part in range(2)
    ]
    for copy in copies:
        copy.start()
    for part, copy in enumerate(copies):
        copy.wait()
        out[:, part * B : part * B + B] = buffer[part].astype(BF16)


def weights_body(coupling, occupation, shifts, weights, weights_turned, factors):
    core = lax.rem(lax.axis_index("energy"), 2)
    first = jnp.where(shifts[0] == 1, 0, 1)
    for at, mode in enumerate((first, 1 - first)):
        matrix = coupling[mode]
        weights[at] = matrix
        weights_turned[at * B : at * B + B, :] = matrix.T
        for side in range(2):
            factor = occupation[mode] + jnp.where(core == side, 1.0, 0.0)
            factors[2 * at + side : 2 * at + side + 1, :] = jnp.full((1, 2 * B), factor, F32)


def prepare_body(pairs, retarded, *refs):
    count = len(pairs)
    rows, turned, buffer, sems = refs[:count], refs[count : 2 * count], refs[-2], refs[-1]
    slab = lax.axis_index("slab")
    away = 1 - 2 * slab
    places = (
        (slab, 2),
        (slab, 2 + away),
        (1 - slab, 2 - away),
        (1 - slab, 2),
        (slab, 2 + 2 * away),
        (1 - slab, 2 + away),
        (1 - slab, 2 + 2 * away),
    )
    copies = []
    for at, t in enumerate(pairs):
        i, j = places[t]
        copies.append(pltpu.make_async_copy(retarded.at[0, i, j], buffer.at[at], sems.at[at]))
        copies[-1].start()
    for at, copy in enumerate(copies):
        copy.wait()
        real = buffer[at, 0]
        imag = buffer[at, 1]
        rows[at][:, :B] = real
        rows[at][:, B:] = imag
        real = real.T
        imag = imag.T
        turned[at][:B, :B] = real
        turned[at][B:, :B] = imag
        turned[at][:B, B:] = -imag
        turned[at][B:, B:] = real


def scatter_body(own, relayed, early, late, weights, weights_turned, factors, out):
    def mixture(first, second, at):
        one = first[...].astype(F32) * factors[at : at + 1, :]
        return (one + second[...].astype(F32) * factors[at + 1 : at + 2, :]).astype(BF16)

    inner_one = dot(weights[0], mixture(own, relayed, 0)).astype(BF16)
    inner_two = dot(weights[1], mixture(early, late, 2)).astype(BF16)
    for part in range(2):
        columns = slice(part * B, part * B + B)
        inner = jnp.concatenate([inner_one[:, columns], inner_two[:, columns]], axis=1)
        out[:, columns] = dot(inner, weights_turned[...]).astype(BF16)


def spread(scattering, full):
    real = scattering[:, :B]
    imag = scattering[:, B:]
    full[:B, :B] = real
    full[:B, B:] = imag
    full[B:, :B] = -imag
    full[B:, B:] = real


def term(rows, full, turned):
    return dot(dot(rows, full[...]).astype(BF16), turned)


def local_body(ballistic, near, far, *refs):
    rows, turned, (out_near, out_far, full) = refs[:4], refs[4:8], refs[8:]
    slab = lax.axis_index("slab")
    for part in range(2):
        columns = slice(part * B, part * B + B)
        out_near[:, columns] = ballistic[0, 1 - slab, part]
        out_far[:, columns] = ballistic[0, slab, part]
    spread(near, full)
    out_near[...] += term(rows[3][...], full, turned[3][...])
    out_far[...] += term(rows[1][...], full, turned[1][...])
    spread(far, full)
    out_near[...] += term(rows[2][...], full, turned[2][...])
    out_far[...] += term(rows[0][...], full, turned[0][...])


def pair_body(total, scattering, rows, turned, out, full):
    spread(scattering, full)
    out[...] = (total[...] + term(rows[...], full, turned[...])).astype(out.dtype)


def last_body(near, far, scattering, rows_far, turned_far, rows_near, turned_near, out, full):
    slab = lax.axis_index("slab")
    spread(scattering, full)
    for total, rows, turned, place in (
        (far, rows_far, turned_far, slab),
        (near, rows_near, turned_near, 1 - slab),
    ):
        result = total[...] + term(rows[...], full, turned[...])
        out[0, place, 0] = result[:, :B]
        out[0, place, 1] = result[:, B:]


def shards(retarded, ballistic, coupling, occupation, shifts):
    energies = lax.axis_size("energy")
    flops = 2 * B * 4 * B * B

    def moves(even, odd):
        steps = [(e, e + (odd if e % 2 else even)) for e in range(energies)]
        return [(a, b) for a, b in steps if 0 <= b < energies]

    early_moves = moves(-2, 2)
    late_moves = moves(2, -2)
    swap_moves = moves(1, -1)

    def shifted(block, pairs):
        return lax.ppermute(block, "energy", pairs)

    def exchange(block):
        early = shifted(block, early_moves)
        late = shifted(block, late_moves)
        own = shifted(block, swap_moves)
        relayed = shifted(early, swap_moves)
        return own, relayed, early, late

    def scatter(*parts):
        return call(
            scatter_body,
            plane(BF16),
            (*parts, weights, weights_turned, factors),
            [VMEM] * 7,
            2 * flops,
            6 << 20,
            12,
        )

    def across(block):
        return lax.ppermute(block, "slab", [(0, 1), (1, 0)])

    def pair(t, total, scattering, dtype):
        return call(
            pair_body,
            plane(dtype),
            (total, scattering, rows[t], turned[t]),
            [VMEM] * 4,
            2 * flops,
            4 << 20,
            12,
            [pltpu.VMEM(SQUARE, BF16)],
        )

    def prepare(pairs):
        count = len(pairs)
        done = call(
            lambda *refs: prepare_body(pairs, *refs),
            [plane(BF16)] * count + [jax.ShapeDtypeStruct(SQUARE, BF16)] * count,
            (pltpu.with_memory_space_constraint(retarded, pltpu.HBM),),
            [HBM],
            0,
            3 * count << 20,
            16,
            [pltpu.VMEM((count, 2, B, B), BF16), pltpu.SemaphoreType.DMA((count,))],
        )
        return done[:count], done[count:]

    def rounded(is_near):
        return call(
            lambda *refs: round_body(is_near, *refs),
            plane(BF16),
            (pltpu.with_memory_space_constraint(ballistic, pltpu.HBM),),
            [HBM],
            0,
            2 << 20,
            4,
            [pltpu.VMEM((2, B, B), F32), pltpu.SemaphoreType.DMA((2,))],
        )

    def weigh():
        return call(
            weights_body,
            [
                jax.ShapeDtypeStruct((2, B, B), BF16),
                jax.ShapeDtypeStruct((2 * B, B), BF16),
                jax.ShapeDtypeStruct((4, 2 * B), F32),
            ],
            (coupling, occupation, shifts),
            [VMEM, SMEM, SMEM],
            0,
            4 << 20,
            4,
        )

    def local(near, far):
        return call(
            local_body,
            [plane(F32), plane(F32)],
            (ballistic, near, far, *rows[:4], *turned[:4]),
            [VMEM] * 11,
            8 * flops,
            14 << 20,
            20,
            [pltpu.VMEM(SQUARE, BF16)],
        )

    def last(near, far, scattering):
        return call(
            last_body,
            jax.ShapeDtypeStruct(ballistic.shape, F32),
            (near, far, scattering, rows[4], turned[4], rows[5], turned[5]),
            [VMEM] * 7,
            4 * flops,
            8 << 20,
            16,
            [pltpu.VMEM(SQUARE, BF16)],
        )

    near = rounded(True)
    far = rounded(False)
    weights, weights_turned, factors = weigh()
    rows, turned = prepare((0, 1, 2, 3))
    more_rows, more_turned = prepare((4, 5, 6))
    rows, turned = rows + more_rows, turned + more_turned
    for tag in ("0", "1"):
        near_parts = exchange(near)
        far_parts = exchange(far)
        scatter_near = scatter(*near_parts)
        scatter_far = scatter(*far_parts)
        other_near = across(scatter_near)
        other_far = across(scatter_far)
        total_near, total_far = local(scatter_near, scatter_far)
        if tag == "0":
            far = pair(4, total_far, other_near, BF16)
            total_near = pair(5, total_near, other_near, F32)
            near = pair(6, total_near, other_far, BF16)
        else:
            total_near = pair(6, total_near, other_far, F32)
            return last(total_near, total_far, other_near)


def solution(mesh):
    return jax.shard_map(
        shards,
        mesh=mesh,
        in_specs=(
            P("energy", "slab", None, None, None, None),
            P("energy", "slab", None, None, None),
            P(),
            P(),
            P(),
        ),
        out_specs=P("energy", "slab", None, None, None),
        check_vma=False,
    )
```
